32 devices in a mesh: shard: 8 (over z, x), context: 2 (over y), tensor: 2 (over core).
Axes of the slice: x: 2, y: 2, z: 4, core: 2. Of those that a mesh axis runs over, the one named last changes fastest.
Arguments:
- block_in: float32 [32, 512, 1088], P(('shard', 'tensor'), 'context'), may hold values from -6 to 6
- cotangent: float32 [32, 512, 1088], P(('shard', 'tensor'), 'context'), may hold values from -6 to 6
- qkv_weight: bfloat16 [1088, 3264], P(('shard', 'tensor')), may hold values from -3 to 3
- out_weight: bfloat16 [1088, 1088], P(('shard', 'tensor')), may hold values from -0.75 to 0.75
- up_weight: bfloat16 [1088, 4352], P('shard', 'tensor'), may hold values from -0.1875 to 0.1875
- down_weight: bfloat16 [4352, 1088], P('tensor', 'shard'), may hold values from -0.09375 to 0.09375
- ln1_gain: bfloat16 [1088], P(('shard', 'tensor')), may hold values from 0.25 to 1.75
- ln1_bias: bfloat16 [1088], P(('shard', 'tensor')), may hold values from -3 to 3
- qv_bias: bfloat16 [2176], P(('shard', 'tensor')), may hold values from -3 to 3
- out_bias: bfloat16 [1088], P(('shard', 'tensor')), may hold values from -3 to 3
- ln2_gain: bfloat16 [1088], P(('shard', 'tensor')), may hold values from 0.25 to 1.75
- ln2_bias: bfloat16 [1088], P(('shard', 'tensor')), may hold values from -3 to 3
- up_bias: bfloat16 [4352], P(('shard', 'tensor')), may hold values from -3 to 3
- down_bias: bfloat16 [1088], P(('shard', 'tensor')), may hold values from -3 to 3
Outputs:
- block_out: float32 [32, 512, 1088], P(('shard', 'tensor'), 'context')
- input_grad: float32 [32, 512, 1088], P(('shard', 'tensor'), 'context')
- qkv_weight_grad: float32 [1088, 3264], P(('shard', 'tensor'))
- out_weight_grad: float32 [1088, 1088], P(('shard', 'tensor'))
- up_weight_grad: float32 [1088, 4352], P('shard', 'tensor')
- down_weight_grad: float32 [4352, 1088], P('tensor', 'shard')
- ln1_gain_grad: float32 [1088], P(('shard', 'tensor'))
- ln1_bias_grad: float32 [1088], P(('shard', 'tensor'))
- qv_bias_grad: float32 [2176], P(('shard', 'tensor'))
- out_bias_grad: float32 [1088], P(('shard', 'tensor'))
- ln2_gain_grad: float32 [1088], P(('shard', 'tensor'))
- ln2_bias_grad: float32 [1088], P(('shard', 'tensor'))
- up_bias_grad: float32 [4352], P(('shard', 'tensor'))
- down_bias_grad: float32 [1088], P(('shard', 'tensor'))
The draws below stay inside these ranges and needn't reach their ends.
All inputs are finite; a program needn't handle non-finite values.
Results may differ from the reference program's by a relative error of at most 0.019.
Values may be sent and summed in bfloat16 or wider, within the bound.
A program may use at most 192 MiB of HBM per device.

```python
import jax
import jax.numpy as jnp
from jax import lax

D = 1088
HEADS = 17
HEAD_DIM = 64
FF = 4352
LEN = 512
SEQS = 32


def draw_qkv_weight(key, part):
    base = jnp.clip(jax.random.normal(key, (D, 3 * D), jnp.float32), -5.0, 5.0) * D ** (-0.5)
    return base.astype(jnp.bfloat16)


def shard_levels(key, extent, split, low, top_value):
    loudness = 1.0
    for dim, parts in split:
        heights = jax.random.uniform(jax.random.fold_in(jax.random.fold_in(key, 6), dim), (parts,), jnp.float32, low / len(split), top_value / len(split))
        loudness = loudness * jnp.repeat(jnp.exp(heights), extent[dim] // parts).reshape((-1,) + (1,) * (len(extent) - 1 - dim))
    return loudness


def normal_values(own_key, extent, deviation, reach, split=(), dtype=jnp.bfloat16):
    level = shard_levels(own_key, extent, split, -0.22, 0.18) if split else 1.0
    values = jax.random.normal(own_key, extent, jnp.float32) * deviation * level
    return jnp.minimum(jnp.maximum(values, -reach), reach).astype(dtype)


def setup_inputs(seed: int = 0) -> dict:
    arg_keys = jax.random.split(jax.random.key(seed), 15)
    block_in = normal_values(arg_keys[0], (SEQS, LEN, D), 1.0, 6.0, ((0, 16), (1, 2)), jnp.float32)
    cotangent = normal_values(arg_keys[1], (SEQS, LEN, D), 1.0, 6.0, ((0, 16), (1, 2)), jnp.float32)
    qkv_weight = draw_qkv_weight(jax.random.fold_in(arg_keys[14], 71), 0)
    out_weight = normal_values(arg_keys[3], (D, D), (D // 16) ** -0.5, 0.75, ((0, 16),))
    up_weight = normal_values(arg_keys[4], (D, FF), D ** -0.5, 0.1875, ((0, 8), (1, 2)))
    down_weight = normal_values(arg_keys[5], (FF, D), FF ** -0.5, 0.09375, ((0, 2), (1, 8)))
    ln1_gain = jnp.clip(1.0 + 0.15 * jax.random.normal(arg_keys[6], (D,), jnp.float32), 0.25, 1.75).astype(jnp.bfloat16)
    ln1_bias = normal_values(arg_keys[7], (D,), 0.5, 3.0, ((0, 16),))
    qv_bias = normal_values(arg_keys[8], (2 * D,), 0.5, 3.0, ((0, 16),))
    out_bias = normal_values(arg_keys[9], (D,), 0.5, 3.0, ((0, 16),))
    ln2_gain = jnp.clip(1.0 + 0.15 * jax.random.normal(arg_keys[10], (D,), jnp.float32), 0.25, 1.75).astype(jnp.bfloat16)
    ln2_bias = normal_values(arg_keys[11], (D,), 0.5, 3.0, ((0, 16),))
    up_bias = normal_values(arg_keys[12], (FF,), 0.5, 3.0, ((0, 16),))
    down_bias = normal_values(arg_keys[13], (D,), 0.5, 3.0, ((0, 16),))
    return {"block_in": block_in, "cotangent": cotangent, "qkv_weight": qkv_weight, "out_weight": out_weight, "up_weight": up_weight, "down_weight": down_weight, "ln1_gain": ln1_gain, "ln1_bias": ln1_bias, "qv_bias": qv_bias, "out_bias": out_bias, "ln2_gain": ln2_gain, "ln2_bias": ln2_bias, "up_bias": up_bias, "down_bias": down_bias}


EPS = 1e-05
GELU_C = 0.7978845608028654
NEG_FILL = -1e+30

def norm_fwd(rows, gain, shift):
    center = rows - lax.optimization_barrier(jnp.mean(rows, -1, keepdims=True))
    rstd = lax.rsqrt(lax.optimization_barrier(jnp.mean(center * center, -1, keepdims=True)) + EPS)
    normed = center * rstd
    return (normed, rstd, normed * gain.astype(jnp.float32) + shift.astype(jnp.float32))

def norm_back(dnorm, normed, rstd):
    mean_a = lax.optimization_barrier(jnp.mean(dnorm, -1, keepdims=True))
    mean_b = lax.optimization_barrier(jnp.mean(dnorm * normed, -1, keepdims=True))
    return rstd * (dnorm - mean_a - normed * mean_b)

def gelu_pair(value):
    inner = GELU_C * (value + 0.044715 * value * value * value)
    tanh_v = jnp.tanh(inner)
    result = 0.5 * value * (1.0 + tanh_v)
    slope = 0.5 * (1.0 + tanh_v) + 0.5 * value * (1.0 - tanh_v * tanh_v) * GELU_C * (1.0 + 3.0 * 0.044715 * value * value)
    return (result, slope)

def split_heads(tensor_in):
    return tensor_in.reshape(tensor_in.shape[0], tensor_in.shape[1], HEADS, HEAD_DIM).astype(jnp.float32)

def masked_scores(queries, keys_all):
    scores = jnp.einsum('sqhd,skhd->shqk', split_heads(queries), split_heads(keys_all)) * HEAD_DIM ** (-0.5)
    qpos = jnp.arange(queries.shape[1])
    kpos = jnp.arange(keys_all.shape[1])
    allowed = kpos[None, :] <= qpos[:, None]
    return jnp.where(allowed[None, None], scores, NEG_FILL)

def block_pass(xb, dyb, weights):
    qkv_weight, out_weight, up_weight, down_weight, ln1_gain, ln1_bias, qv_bias, out_bias, ln2_gain, ln2_bias, up_bias, down_bias = weights
    count = xb.shape[0]
    rows = xb.reshape(-1, D)
    normed1, rstd1, pre1 = norm_fwd(rows, ln1_gain, ln1_bias)
    act1 = pre1.astype(jnp.bfloat16)
    qvb = qv_bias.astype(jnp.float32)
    qkv_bias = jnp.concatenate([qvb[:D], jnp.zeros((D,), jnp.float32), qvb[D:]])
    qkv = jnp.dot(act1, qkv_weight, preferred_element_type=jnp.float32) + qkv_bias
    queries = qkv[:, :D].astype(jnp.bfloat16).reshape(count, LEN, D)
    keys_all = qkv[:, D:2 * D].astype(jnp.bfloat16).reshape(count, LEN, D)
    values_all = qkv[:, 2 * D:].astype(jnp.bfloat16).reshape(count, LEN, D)
    scores = masked_scores(queries, keys_all)
    top = lax.optimization_barrier(jnp.max(scores, -1, keepdims=True))
    lse = top + jnp.log(lax.optimization_barrier(jnp.sum(jnp.exp(scores - top), -1, keepdims=True)))
    probs = jnp.exp(scores - lse).astype(jnp.bfloat16)
    attended = jnp.einsum('shqk,skhd->sqhd', probs.astype(jnp.float32), split_heads(values_all))
    attended = attended.reshape(-1, D).astype(jnp.bfloat16)
    resid = rows + jnp.dot(attended, out_weight, preferred_element_type=jnp.float32) + out_bias.astype(jnp.float32)
    normed2, rstd2, pre2 = norm_fwd(resid, ln2_gain, ln2_bias)
    act2 = pre2.astype(jnp.bfloat16)
    pre = jnp.dot(act2, up_weight, preferred_element_type=jnp.float32) + up_bias.astype(jnp.float32)
    hval, slope = gelu_pair(pre)
    hidden = hval.astype(jnp.bfloat16)
    block_out = resid + jnp.dot(hidden, down_weight, preferred_element_type=jnp.float32) + down_bias.astype(jnp.float32)
    cot = dyb.reshape(-1, D)
    g_down_bias = lax.optimization_barrier(jnp.sum(cot, 0))
    cot_low = cot.astype(jnp.bfloat16)
    g_down = jnp.dot(hidden.T, cot_low, preferred_element_type=jnp.float32)
    pre_grad = jnp.dot(cot_low, down_weight.T, preferred_element_type=jnp.float32) * slope
    g_up_bias = lax.optimization_barrier(jnp.sum(pre_grad, 0))
    pre_low = pre_grad.astype(jnp.bfloat16)
    g_up = jnp.dot(act2.T, pre_low, preferred_element_type=jnp.float32)
    act2_grad = jnp.dot(pre_low, up_weight.T, preferred_element_type=jnp.float32)
    g_gain2 = lax.optimization_barrier(jnp.sum(act2_grad * normed2, 0))
    g_shift2 = lax.optimization_barrier(jnp.sum(act2_grad, 0))
    resid_grad = cot + norm_back(act2_grad * ln2_gain.astype(jnp.float32), normed2, rstd2)
    g_out_bias = lax.optimization_barrier(jnp.sum(resid_grad, 0))
    resid_low = resid_grad.astype(jnp.bfloat16)
    g_out = jnp.dot(attended.T, resid_low, preferred_element_type=jnp.float32)
    attended_grad = jnp.dot(resid_low, out_weight.T, preferred_element_type=jnp.float32).astype(jnp.bfloat16)
    attended_grad = attended_grad.reshape(count, LEN, D)
    pf = jnp.exp(masked_scores(queries, keys_all) - lse)
    probs_low = pf.astype(jnp.bfloat16)
    dprobs = jnp.einsum('sqhd,skhd->shqk', split_heads(attended_grad), split_heads(values_all))
    delta = lax.optimization_barrier(jnp.sum(pf * dprobs, -1, keepdims=True))
    dscore = (pf * (dprobs - delta)).astype(jnp.bfloat16).astype(jnp.float32)
    scale = HEAD_DIM ** (-0.5)
    query_grad = jnp.einsum('shqk,skhd->sqhd', dscore, split_heads(keys_all)) * scale
    key_grad = jnp.einsum('shqk,sqhd->skhd', dscore, split_heads(queries)) * scale
    value_grad = jnp.einsum('shqk,sqhd->skhd', probs_low.astype(jnp.float32), split_heads(attended_grad))
    query_grad = query_grad.reshape(-1, D)
    key_grad = key_grad.reshape(-1, D)
    value_grad = value_grad.reshape(-1, D)
    g_qv_bias = jnp.concatenate([lax.optimization_barrier(jnp.sum(query_grad, 0)), lax.optimization_barrier(jnp.sum(value_grad, 0))])
    qkv_low = jnp.concatenate([query_grad, key_grad, value_grad], 1).astype(jnp.bfloat16)
    g_qkv = jnp.dot(act1.T, qkv_low, preferred_element_type=jnp.float32)
    act1_grad = jnp.dot(qkv_low, qkv_weight.T, preferred_element_type=jnp.float32)
    g_gain1 = lax.optimization_barrier(jnp.sum(act1_grad * normed1, 0))
    g_shift1 = lax.optimization_barrier(jnp.sum(act1_grad, 0))
    input_grad = resid_grad + norm_back(act1_grad * ln1_gain.astype(jnp.float32), normed1, rstd1)
    grads = (g_qkv, g_out, g_up, g_down, g_gain1, g_shift1, g_qv_bias, g_out_bias, g_gain2, g_shift2, g_up_bias, g_down_bias)
    return (block_out.reshape(count, LEN, D), input_grad.reshape(count, LEN, D), grads)

def reference(block_in, cotangent, qkv_weight, out_weight, up_weight, down_weight, ln1_gain, ln1_bias, qv_bias, out_bias, ln2_gain, ln2_bias, up_bias, down_bias):
    weights = (qkv_weight, out_weight, up_weight, down_weight, ln1_gain, ln1_bias, qv_bias, out_bias, ln2_gain, ln2_bias, up_bias, down_bias)
    group = 8
    blocks = SEQS // group
    xs = (block_in.reshape(blocks, group, LEN, D), cotangent.reshape(blocks, group, LEN, D))
    start = (jnp.zeros((D, 3 * D), jnp.float32), jnp.zeros((D, D), jnp.float32), jnp.zeros((D, FF), jnp.float32), jnp.zeros((FF, D), jnp.float32), jnp.zeros((D,), jnp.float32), jnp.zeros((D,), jnp.float32), jnp.zeros((2 * D,), jnp.float32), jnp.zeros((D,), jnp.float32), jnp.zeros((D,), jnp.float32), jnp.zeros((D,), jnp.float32), jnp.zeros((FF,), jnp.float32), jnp.zeros((D,), jnp.float32))

    def step_fn(carry, pair):
        out_b, grad_b, grads = block_pass(pair[0], pair[1], weights)
        return (tuple((c + g for c, g in zip(carry, grads))), (out_b, grad_b))
    totals, outs = lax.scan(step_fn, start, xs)
    block_out = outs[0].reshape(SEQS, LEN, D)
    input_grad = outs[1].reshape(SEQS, LEN, D)
    return (block_out, input_grad, totals[0], totals[1], totals[2], totals[3], totals[4], totals[5], totals[6], totals[7], totals[8], totals[9], totals[10], totals[11])
```

```python
import functools

import jax
import jax.numpy as jnp
from jax import lax
from jax.sharding import PartitionSpec as P

HEADS = 17
HEAD_DIM = 64


EPS = 1e-05
GELU_C = 0.7978845608028654
NEG_FILL = -1e30


def norm_fwd(rows, gain, shift):
    center = rows - jnp.mean(rows, -1, keepdims=True)
    rstd = lax.rsqrt(jnp.mean(center * center, -1, keepdims=True) + EPS)
    normed = center * rstd
    return (normed, rstd, normed * gain.astype(jnp.float32) + shift.astype(jnp.float32))


def norm_back(dnorm, normed, rstd):
    mean_a = jnp.mean(dnorm, -1, keepdims=True)
    mean_b = jnp.mean(dnorm * normed, -1, keepdims=True)
    return rstd * (dnorm - mean_a - normed * mean_b)


def gelu_pair(value):
    inner = GELU_C * (value + 0.044715 * value * value * value)
    tanh_v = jnp.tanh(inner)
    result = 0.5 * value * (1.0 + tanh_v)
    slope = 0.5 * (1.0 + tanh_v) + 0.5 * value * (1.0 - tanh_v * tanh_v) * GELU_C * (
        1.0 + 3.0 * 0.044715 * value * value
    )
    return (result, slope)


def split_heads(tensor_in):
    return tensor_in.reshape(tensor_in.shape[0], tensor_in.shape[1], HEADS, HEAD_DIM)


def masked_scores(queries, keys_all, q_start):
    scores = jnp.einsum(
        "sqhd,skhd->shqk",
        split_heads(queries),
        split_heads(keys_all),
        preferred_element_type=jnp.float32,
    ) * HEAD_DIM ** (-0.5)
    qpos = q_start + jnp.arange(queries.shape[1])
    kpos = jnp.arange(keys_all.shape[1])
    allowed = kpos[None, :] <= qpos[:, None]
    return jnp.where(allowed[None, None], scores, NEG_FILL)


def on_device(
    block_in,
    cotangent,
    qkv_weight,
    out_weight,
    up_weight,
    down_weight,
    ln1_gain,
    ln1_bias,
    qv_bias,
    out_bias,
    ln2_gain,
    ln2_bias,
    up_bias,
    down_bias,
):
    seqs_loc, rows_q, width = block_in.shape
    qkv_full, out_full, gain1, shift1, qvb, outb, gain2, shift2, upb_all, downb = (
        lax.all_gather(qkv_weight, ("shard", "tensor"), axis=0, tiled=True),
        lax.all_gather(out_weight, ("shard", "tensor"), axis=0, tiled=True),
        lax.all_gather(ln1_gain, ("shard", "tensor"), axis=0, tiled=True),
        lax.all_gather(ln1_bias, ("shard", "tensor"), axis=0, tiled=True),
        lax.all_gather(qv_bias, ("shard", "tensor"), axis=0, tiled=True),
        lax.all_gather(out_bias, ("shard", "tensor"), axis=0, tiled=True),
        lax.all_gather(ln2_gain, ("shard", "tensor"), axis=0, tiled=True),
        lax.all_gather(ln2_bias, ("shard", "tensor"), axis=0, tiled=True),
        lax.all_gather(up_bias, ("shard", "tensor"), axis=0, tiled=True),
        lax.all_gather(down_bias, ("shard", "tensor"), axis=0, tiled=True),
    )
    up_full, down_full = (
        lax.all_gather(up_weight, "shard", axis=0, tiled=True),
        lax.all_gather(down_weight, "shard", axis=1, tiled=True),
    )
    hidden_loc = up_full.shape[1]
    tensor_pos = lax.axis_index("tensor")
    upb = lax.dynamic_slice_in_dim(upb_all, tensor_pos * hidden_loc, hidden_loc).astype(jnp.float32)
    rows = block_in.reshape(-1, width)
    normed1, rstd1, pre1 = norm_fwd(rows, gain1, shift1)
    act1 = pre1.astype(jnp.bfloat16)
    qv_wide = qvb.astype(jnp.float32)
    qkv_bias = jnp.concatenate([qv_wide[:width], jnp.zeros((width,), jnp.float32), qv_wide[width:]])
    qkv = jnp.dot(act1, qkv_full, preferred_element_type=jnp.float32) + qkv_bias
    queries = qkv[:, :width].astype(jnp.bfloat16).reshape(seqs_loc, rows_q, width)
    keys_loc = qkv[:, width : 2 * width].astype(jnp.bfloat16).reshape(seqs_loc, rows_q, width)
    values_loc = qkv[:, 2 * width :].astype(jnp.bfloat16).reshape(seqs_loc, rows_q, width)
    keys_all, values_all = (
        lax.all_gather(keys_loc, "context", axis=1, tiled=True),
        lax.all_gather(values_loc, "context", axis=1, tiled=True),
    )
    keys_len = keys_all.shape[1]
    q_start = lax.axis_index("context") * rows_q
    scores = masked_scores(queries, keys_all, q_start)
    top = jnp.max(scores, -1, keepdims=True)
    lse = top + jnp.log(jnp.sum(jnp.exp(scores - top), -1, keepdims=True))
    probs = jnp.exp(scores - lse).astype(jnp.bfloat16)
    attended = jnp.einsum(
        "shqk,skhd->sqhd", probs, split_heads(values_all), preferred_element_type=jnp.float32
    )
    attended = attended.reshape(-1, width).astype(jnp.bfloat16)
    resid = (
        rows
        + jnp.dot(attended, out_full, preferred_element_type=jnp.float32)
        + outb.astype(jnp.float32)
    )
    normed2, rstd2, pre2 = norm_fwd(resid, gain2, shift2)
    act2 = pre2.astype(jnp.bfloat16).reshape(seqs_loc, rows_q, width)
    act2_all = lax.all_gather(act2, "tensor", axis=0, tiled=True).reshape(-1, width)
    pre = jnp.dot(act2_all, up_full, preferred_element_type=jnp.float32) + upb
    hval, slope = gelu_pair(pre)
    hidden = hval.astype(jnp.bfloat16)
    partial_out = jnp.dot(hidden, down_full, preferred_element_type=jnp.float32).reshape(
        -1, rows_q, width
    )
    mlp_out = (
        lax.psum_scatter(
            partial_out.astype(jnp.bfloat16), "tensor", scatter_dimension=0, tiled=True
        )
        .astype(jnp.float32)
        .reshape(-1, width)
    )
    block_out = resid + mlp_out + downb.astype(jnp.float32)
    cot = cotangent.reshape(-1, width)
    g_down_bias = jnp.sum(cot, 0)
    cot_all = lax.all_gather(cotangent.astype(jnp.bfloat16), "tensor", axis=0, tiled=True).reshape(
        -1, width
    )
    up_back, down_back = (up_full, down_full)
    qkv_back, out_back = (qkv_full, out_full)
    g_down_t = jnp.dot(cot_all.T, hidden, preferred_element_type=jnp.float32)
    pre_grad = jnp.dot(cot_all, down_back.T, preferred_element_type=jnp.float32) * slope
    g_up_loc = jnp.sum(pre_grad, 0)
    pre_low = pre_grad.astype(jnp.bfloat16)
    g_up = jnp.dot(act2_all.T, pre_low, preferred_element_type=jnp.float32)
    act2_part = jnp.dot(pre_low, up_back.T, preferred_element_type=jnp.float32).reshape(
        -1, rows_q, width
    )
    act2_grad = (
        lax.psum_scatter(act2_part.astype(jnp.bfloat16), "tensor", scatter_dimension=0, tiled=True)
        .astype(jnp.float32)
        .reshape(-1, width)
    )
    g_gain2 = jnp.sum(act2_grad * normed2, 0)
    g_shift2 = jnp.sum(act2_grad, 0)
    resid_grad = cot + norm_back(act2_grad * gain2.astype(jnp.float32), normed2, rstd2)
    g_out_bias = jnp.sum(resid_grad, 0)
    resid_low = resid_grad.astype(jnp.bfloat16)
    g_out = jnp.dot(attended.T, resid_low, preferred_element_type=jnp.float32)
    attended_grad = jnp.dot(resid_low, out_back.T, preferred_element_type=jnp.float32).astype(
        jnp.bfloat16
    )
    attended_grad = attended_grad.reshape(seqs_loc, rows_q, width)
    pf = jnp.exp(masked_scores(queries, keys_all, q_start) - lse)
    probs_low = pf.astype(jnp.bfloat16)
    dprobs = jnp.einsum(
        "sqhd,skhd->shqk",
        split_heads(attended_grad),
        split_heads(values_all),
        preferred_element_type=jnp.float32,
    )
    delta = jnp.sum(pf * dprobs, -1, keepdims=True)
    dscore = (pf * (dprobs - delta)).astype(jnp.bfloat16)
    scale = HEAD_DIM ** (-0.5)
    query_grad = (
        jnp.einsum(
            "shqk,skhd->sqhd", dscore, split_heads(keys_all), preferred_element_type=jnp.float32
        )
        * scale
    )
    key_full = (
        jnp.einsum(
            "shqk,sqhd->skhd", dscore, split_heads(queries), preferred_element_type=jnp.float32
        )
        * scale
    )
    value_full = jnp.einsum(
        "shqk,sqhd->skhd", probs_low, split_heads(attended_grad), preferred_element_type=jnp.float32
    )
    kv_full = jnp.concatenate(
        [
            key_full.reshape(seqs_loc, keys_len, width),
            value_full.reshape(seqs_loc, keys_len, width),
        ],
        2,
    )
    kv_grad = lax.psum_scatter(
        kv_full.astype(jnp.bfloat16), "context", scatter_dimension=1, tiled=True
    ).astype(jnp.float32)
    query_grad = query_grad.reshape(-1, width)
    key_grad = kv_grad[:, :, :width].reshape(-1, width)
    value_grad = kv_grad[:, :, width:].reshape(-1, width)
    g_qv_bias = jnp.concatenate([jnp.sum(query_grad, 0), jnp.sum(value_grad, 0)])
    qkv_low = jnp.concatenate([query_grad, key_grad, value_grad], 1).astype(jnp.bfloat16)
    g_qkv = jnp.dot(act1.T, qkv_low, preferred_element_type=jnp.float32)
    act1_grad = jnp.dot(qkv_low, qkv_back.T, preferred_element_type=jnp.float32)
    g_gain1 = jnp.sum(act1_grad * normed1, 0)
    g_shift1 = jnp.sum(act1_grad, 0)
    input_grad = resid_grad + norm_back(act1_grad * gain1.astype(jnp.float32), normed1, rstd1)
    g_up_bias = lax.dynamic_update_slice_in_dim(
        jnp.zeros((upb_all.shape[0],), jnp.float32), g_up_loc, tensor_pos * hidden_loc, 0
    )
    small_cols = jnp.stack([g_gain1, g_shift1, g_out_bias, g_gain2, g_shift2, g_down_bias], 1)
    attn_stack = jnp.concatenate(
        [g_qkv, g_out, small_cols, g_qv_bias.reshape(width, 2), g_up_bias.reshape(width, -1)], 1
    )
    mlp_stack = jnp.concatenate([g_up, g_down_t], 1)
    s_attn = lax.psum_scatter(
        attn_stack.astype(jnp.bfloat16), ("shard", "tensor"), scatter_dimension=0, tiled=True
    )
    s_mlp = lax.psum_scatter(
        mlp_stack.astype(jnp.bfloat16), "shard", scatter_dimension=0, tiled=True
    )
    t_attn, t_mlp = (
        lax.psum(s_attn, "context").astype(jnp.float32),
        lax.psum(s_mlp, "context").astype(jnp.float32),
    )
    base = 4 * width
    t_qkv = t_attn[:, : 3 * width]
    t_out = t_attn[:, 3 * width : base]
    t_gain1 = t_attn[:, base]
    t_shift1 = t_attn[:, base + 1]
    t_outb = t_attn[:, base + 2]
    t_gain2 = t_attn[:, base + 3]
    t_shift2 = t_attn[:, base + 4]
    t_downb = t_attn[:, base + 5]
    t_qvb = t_attn[:, base + 6 : base + 8].reshape(-1)
    t_upb = t_attn[:, base + 8 :].reshape(-1)
    t_up = t_mlp[:, :hidden_loc]
    t_down = t_mlp[:, hidden_loc:].T
    return (
        block_out.reshape(seqs_loc, rows_q, width),
        input_grad.reshape(seqs_loc, rows_q, width),
        t_qkv,
        t_out,
        t_up,
        t_down,
        t_gain1,
        t_shift1,
        t_qvb,
        t_outb,
        t_gain2,
        t_shift2,
        t_upb,
        t_downb,
    )


def swap(value, axis, size, bit=1):
    return lax.ppermute(value, axis, [(i, i ^ bit) for i in range(size)])


def pick(value, index, dim):
    return lax.dynamic_index_in_dim(value, index, dim, keepdims=False)


def wide(value):
    return value.astype(jnp.float32)


def halve(value, dim, axis, size, bit=1):
    mine = (lax.axis_index(axis) // bit) % 2
    got = swap(pick(value, 1 - mine, dim), axis, size, bit)
    return (wide(pick(value, mine, dim)) + wide(got)).astype(jnp.bfloat16)


def pair(first, second, flag, dim):
    return jnp.where(
        flag == 0, jnp.concatenate([first, second], dim), jnp.concatenate([second, first], dim)
    )


def reduce_owned(grad, shards, context_first):
    blocks, keep_rows, cols = grad.shape
    stages = shards.bit_length() - 1
    grad = grad.reshape(*([2] * stages), 2, 2, keep_rows, cols)
    grad = halve(grad, stages, "tensor", 2)
    if context_first:
        grad = halve(grad, stages, "context", 2)
        grad = halve(grad, stages - 1, "shard", shards)
    else:
        grad = halve(grad, stages - 1, "shard", shards)
        grad = halve(grad, stages - 1, "context", 2)
    for left in range(stages - 1, 0, -1):
        grad = halve(grad, 0, "shard", shards, 2**left)
    return grad


def whole_rows(part, rows, flag):
    part = part[:rows]
    return wide(pair(part, swap(part, "context", 2), flag, 0))


def on_device_pairs(
    shards,
    block_in,
    cotangent,
    qkv_weight,
    out_weight,
    up_weight,
    down_weight,
    ln1_gain,
    ln1_bias,
    qv_bias,
    out_bias,
    ln2_gain,
    ln2_bias,
    up_bias,
    down_bias,
):
    f32, bf16 = jnp.float32, jnp.bfloat16
    _, rows_half, width = block_in.shape
    length = 2 * rows_half
    owners = 2 * shards
    own = width // owners
    ctx, tpos, spos = (lax.axis_index(a) for a in ("context", "tensor", "shard"))
    dot = functools.partial(jnp.dot, preferred_element_type=f32)

    def to_sequence(value):
        return pair(pick(value, ctx, 0), swap(pick(value, 1 - ctx, 0), "context", 2), ctx, 0)

    def from_sequence(value):
        value = value.reshape(2, rows_half, width)
        mine, got = pick(value, ctx, 0), swap(pick(value, 1 - ctx, 0).astype(bf16), "context", 2)
        return pair(mine[None], got[None].astype(f32), ctx, 0)

    smalls = [ln1_gain, ln1_bias, out_bias, ln2_gain, ln2_bias, down_bias, qv_bias, up_bias]
    small = jnp.concatenate(smalls)
    small = jnp.pad(small, (0, qkv_weight.shape[1] - small.shape[0]))[None]
    packed = jnp.concatenate([qkv_weight, small], 0)[None]
    packed_all = lax.all_gather(packed, ("shard", "tensor"), axis=0, tiled=True)
    rows = to_sequence(block_in)
    out_full = lax.all_gather(out_weight[None], ("shard", "tensor"), axis=0, tiled=True)
    out_full = out_full.reshape(width, width)
    hid = up_weight.shape[1] // 2
    up_part = lax.dynamic_slice_in_dim(up_weight, ctx * hid, hid, 1)
    down_part = lax.dynamic_slice_in_dim(down_weight, ctx * hid, hid, 0).T
    up_full = lax.all_gather(up_part, "shard", axis=0, tiled=True)
    down_t = lax.all_gather(down_part, "shard", axis=0, tiled=True)
    qkv_full = packed_all[:, :own].reshape(width, -1)
    small_all = packed_all[:, own]
    gathered, at = [], 0
    for s in smalls:
        gathered.append(small_all[:, at : at + s.shape[0]].reshape(-1))
        at += s.shape[0]
    gain1, shift1, outb, gain2, shift2, downb, qvb, upb_all = gathered
    upb = wide(lax.dynamic_slice_in_dim(upb_all, (tpos * 2 + ctx) * hid, hid))

    normed1, rstd1, pre1 = norm_fwd(rows, gain1, shift1)
    act1 = pre1.astype(bf16)
    qv_wide = wide(qvb)
    qkv_bias = jnp.concatenate([qv_wide[:width], jnp.zeros((width,), f32), qv_wide[width:]])
    qkv = (dot(act1, qkv_full) + qkv_bias).astype(bf16)
    queries = qkv[None, :, :width]
    keys = qkv[None, :, width : 2 * width]
    values = qkv[None, :, 2 * width :]
    scores = masked_scores(queries, keys, 0)
    top = jnp.max(scores, -1, keepdims=True)
    lse = top + jnp.log(jnp.sum(jnp.exp(scores - top), -1, keepdims=True))
    probs = jnp.exp(scores - lse).astype(bf16)
    attended = jnp.einsum("shqk,skhd->sqhd", probs, split_heads(values), preferred_element_type=f32)
    attended = attended.reshape(-1, width).astype(bf16)
    resid = rows + dot(attended, out_full) + wide(outb)
    normed2, rstd2, pre2 = norm_fwd(resid, gain2, shift2)

    def spread(value):
        near = jnp.concatenate([value, swap(value, "tensor", 2)], 0)
        far = swap(value, "context", 2)
        return near, jnp.concatenate([far, swap(far, "tensor", 2)], 0)

    def collect(near, far):
        near, far = near.reshape(2, length, width), far.reshape(2, length, width)
        far = far[0] + wide(swap(far[1].astype(bf16), "tensor", 2))
        far = wide(swap(far.astype(bf16), "context", 2))
        return near[0] + wide(swap(near[1].astype(bf16), "tensor", 2)) + far

    def against(left, right):
        return lax.dot_general(left, right, (((1,), (1,)), ((), ())), preferred_element_type=f32)

    def over_tokens(left, right):
        return lax.dot_general(left, right, (((0,), (0,)), ((), ())), preferred_element_type=f32)

    cot = to_sequence(cotangent)
    cot_sets = spread(cot.astype(bf16))
    act2_sets = spread(pre2.astype(bf16))
    hiddens, slopes = [], []
    for act in act2_sets:
        hval, slope = gelu_pair(dot(act, up_full) + upb)
        hiddens.append(hval.astype(bf16))
        slopes.append(slope)
    pre_grads = [dot(c, down_t) * s for c, s in zip(cot_sets, slopes)]
    g_up_loc = sum(jnp.sum(p, 0) for p in pre_grads)
    pre_lows = [p.astype(bf16) for p in pre_grads]
    act2_grad = collect(*[against(p, up_full) for p in pre_lows])
    cot_cat = jnp.concatenate(cot_sets, 0)
    act2_cat = jnp.concatenate(act2_sets, 0)
    g_down_t = over_tokens(cot_cat, jnp.concatenate(hiddens, 0)).astype(bf16)
    g_up = over_tokens(act2_cat, jnp.concatenate(pre_lows, 0)).astype(bf16)
    s_down = lax.psum_scatter(g_down_t, "shard", scatter_dimension=0, tiled=True)
    s_up = lax.psum_scatter(g_up, "shard", scatter_dimension=0, tiled=True)
    mlp_out = collect(*[against(h, down_t) for h in hiddens])
    block_out = from_sequence(resid + mlp_out + wide(downb))

    g_down_bias = jnp.sum(cot, 0)
    g_gain2 = jnp.sum(act2_grad * normed2, 0)
    g_shift2 = jnp.sum(act2_grad, 0)
    resid_grad = cot + norm_back(act2_grad * wide(gain2), normed2, rstd2)
    g_out_bias = jnp.sum(resid_grad, 0)
    resid_low = resid_grad.astype(bf16)
    half = own // 2
    pad_rows = -half % 8

    def in_blocks(value):
        value = value.reshape(length, 2 * owners, half)
        return jnp.pad(value, ((0, 0), (0, 0), (0, pad_rows))).reshape(length, -1)

    def owned(left, right, context_first):
        grad = over_tokens(left, right).astype(bf16)
        return reduce_owned(
            grad.reshape(2 * owners, half + pad_rows, -1), shards, context_first
        )

    s_out = owned(in_blocks(attended), resid_low, True)
    attended_grad = against(resid_low, out_full).astype(bf16)[None]
    pf = jnp.exp(masked_scores(queries, keys, 0) - lse)
    probs_low = pf.astype(bf16)
    dprobs = jnp.einsum(
        "sqhd,skhd->shqk",
        split_heads(attended_grad),
        split_heads(values),
        preferred_element_type=f32,
    )
    delta = jnp.sum(pf * dprobs, -1, keepdims=True)
    dscore = (pf * (dprobs - delta)).astype(bf16)
    scale = HEAD_DIM ** (-0.5)
    query_grad = scale * jnp.einsum(
        "shqk,skhd->sqhd", dscore, split_heads(keys), preferred_element_type=f32
    )
    key_grad = scale * jnp.einsum(
        "shqk,sqhd->skhd", dscore, split_heads(queries), preferred_element_type=f32
    )
    value_grad = jnp.einsum(
        "shqk,sqhd->skhd", probs_low, split_heads(attended_grad), preferred_element_type=f32
    )
    query_grad, key_grad, value_grad = (
        g.reshape(-1, width) for g in (query_grad, key_grad, value_grad)
    )
    g_qv_bias = jnp.concatenate([jnp.sum(query_grad, 0), jnp.sum(value_grad, 0)])
    qkv_low = jnp.concatenate([query_grad, key_grad, value_grad], 1).astype(bf16)
    act1_blocks = in_blocks(act1)
    cut = -(-qkv_low.shape[1] // 256) * 128
    s_qkv = [
        owned(act1_blocks, qkv_low[:, :cut], False),
        owned(act1_blocks, qkv_low[:, cut:], True),
    ]
    act1_grad = against(qkv_low, qkv_full)
    g_gain1 = jnp.sum(act1_grad * normed1, 0)
    g_shift1 = jnp.sum(act1_grad, 0)
    input_grad = resid_grad + norm_back(act1_grad * wide(gain1), normed1, rstd1)
    input_grad = from_sequence(input_grad)
    g_up_bias = lax.dynamic_update_slice_in_dim(
        jnp.zeros((upb_all.shape[0],), f32), g_up_loc, (tpos * 2 + ctx) * hid, 0
    )
    g_smalls = [
        g_gain1, g_shift1, g_out_bias, g_gain2, g_shift2, g_down_bias, g_qv_bias, g_up_bias
    ]
    g_small = jnp.concatenate([g.reshape(owners, -1) for g in g_smalls], 1)
    g_small = pick(lax.psum(g_small, ("shard", "context", "tensor")), spos * 2 + tpos, 0)
    t_small, at = [], 0
    for s in smalls:
        t_small.append(g_small[at : at + s.shape[0]])
        at += s.shape[0]
    t_gain1, t_shift1, t_outb, t_gain2, t_shift2, t_downb, t_qvb, t_upb = t_small
    t_qkv = jnp.concatenate([whole_rows(s, half, ctx) for s in s_qkv], 1)
    t_out = whole_rows(s_out, half, ctx)
    t_up = wide(pair(s_up, swap(s_up, "context", 2), ctx, 1))
    t_down = wide(pair(s_down, swap(s_down, "context", 2), ctx, 1)).T
    return (
        block_out,
        input_grad,
        t_qkv,
        t_out,
        t_up,
        t_down,
        t_gain1,
        t_shift1,
        t_qvb,
        t_outb,
        t_gain2,
        t_shift2,
        t_upb,
        t_downb,
    )


def device_step(mesh):
    shards = mesh.shape["shard"]
    paired = mesh.shape["context"] == 2 and mesh.shape["tensor"] == 2
    paired = paired and shards > 1 and shards & (shards - 1) == 0

    def step(block_in, *rest):
        width = block_in.shape[2]
        if paired and block_in.shape[0] == 2 and width % (4 * shards) == 0:
            return on_device_pairs(shards, block_in, *rest)
        return on_device(block_in, *rest)

    return step


def solution(mesh):
    return jax.shard_map(
        device_step(mesh),
        mesh=mesh,
        in_specs=(
            P(("shard", "tensor"), "context", None),
            P(("shard", "tensor"), "context", None),
            P(("shard", "tensor"), None),
            P(("shard", "tensor"), None),
            P("shard", "tensor"),
            P("tensor", "shard"),
            P(("shard", "tensor")),
            P(("shard", "tensor")),
            P(("shard", "tensor")),
            P(("shard", "tensor")),
            P(("shard", "tensor")),
            P(("shard", "tensor")),
            P(("shard", "tensor")),
            P(("shard", "tensor")),
        ),
        out_specs=(
            P(("shard", "tensor"), "context", None),
            P(("shard", "tensor"), "context", None),
            P(("shard", "tensor"), None),
            P(("shard", "tensor"), None),
            P("shard", "tensor"),
            P("tensor", "shard"),
            P(("shard", "tensor")),
            P(("shard", "tensor")),
            P(("shard", "tensor")),
            P(("shard", "tensor")),
            P(("shard", "tensor")),
            P(("shard", "tensor")),
            P(("shard", "tensor")),
            P(("shard", "tensor")),
        ),
        check_vma=False,
    )
```

```python
import functools

import jax
import jax.numpy as jnp
from jax import lax
from jax.sharding import PartitionSpec as P

HEADS = 17
HEAD_DIM = 64


EPS = 1e-05
GELU_C = 0.7978845608028654
NEG_FILL = -1e30


def norm_fwd(rows, gain, shift):
    center = rows - jnp.mean(rows, -1, keepdims=True)
    rstd = lax.rsqrt(jnp.mean(center * center, -1, keepdims=True) + EPS)
    normed = center * rstd
    return (normed, rstd, normed * gain.astype(jnp.float32) + shift.astype(jnp.float32))


def norm_back(dnorm, normed, rstd):
    mean_a = jnp.mean(dnorm, -1, keepdims=True)
    mean_b = jnp.mean(dnorm * normed, -1, keepdims=True)
    return rstd * (dnorm - mean_a - normed * mean_b)


def gelu_pair(value):
    inner = GELU_C * (value + 0.044715 * value * value * value)
    tanh_v = jnp.tanh(inner)
    result = 0.5 * value * (1.0 + tanh_v)
    slope = 0.5 * (1.0 + tanh_v) + 0.5 * value * (1.0 - tanh_v * tanh_v) * GELU_C * (
        1.0 + 3.0 * 0.044715 * value * value
    )
    return (result, slope)


def split_heads(tensor_in):
    return tensor_in.reshape(tensor_in.shape[0], tensor_in.shape[1], HEADS, HEAD_DIM)


def masked_scores(queries, keys_all, q_start):
    scores = jnp.einsum(
        "sqhd,skhd->shqk",
        split_heads(queries),
        split_heads(keys_all),
        preferred_element_type=jnp.float32,
    ) * HEAD_DIM ** (-0.5)
    qpos = q_start + jnp.arange(queries.shape[1])
    kpos = jnp.arange(keys_all.shape[1])
    allowed = kpos[None, :] <= qpos[:, None]
    return jnp.where(allowed[None, None], scores, NEG_FILL)


def on_device(
    block_in,
    cotangent,
    qkv_weight,
    out_weight,
    up_weight,
    down_weight,
    ln1_gain,
    ln1_bias,
    qv_bias,
    out_bias,
    ln2_gain,
    ln2_bias,
    up_bias,
    down_bias,
):
    seqs_loc, rows_q, width = block_in.shape
    qkv_full, out_full, gain1, shift1, qvb, outb, gain2, shift2, upb_all, downb = (
        lax.all_gather(qkv_weight, ("shard", "tensor"), axis=0, tiled=True),
        lax.all_gather(out_weight, ("shard", "tensor"), axis=0, tiled=True),
        lax.all_gather(ln1_gain, ("shard", "tensor"), axis=0, tiled=True),
        lax.all_gather(ln1_bias, ("shard", "tensor"), axis=0, tiled=True),
        lax.all_gather(qv_bias, ("shard", "tensor"), axis=0, tiled=True),
        lax.all_gather(out_bias, ("shard", "tensor"), axis=0, tiled=True),
        lax.all_gather(ln2_gain, ("shard", "tensor"), axis=0, tiled=True),
        lax.all_gather(ln2_bias, ("shard", "tensor"), axis=0, tiled=True),
        lax.all_gather(up_bias, ("shard", "tensor"), axis=0, tiled=True),
        lax.all_gather(down_bias, ("shard", "tensor"), axis=0, tiled=True),
    )
    up_full, down_full = (
        lax.all_gather(up_weight, "shard", axis=0, tiled=True),
        lax.all_gather(down_weight, "shard", axis=1, tiled=True),
    )
    hidden_loc = up_full.shape[1]
    tensor_pos = lax.axis_index("tensor")
    upb = lax.dynamic_slice_in_dim(upb_all, tensor_pos * hidden_loc, hidden_loc).astype(jnp.float32)
    rows = block_in.reshape(-1, width)
    normed1, rstd1, pre1 = norm_fwd(rows, gain1, shift1)
    act1 = pre1.astype(jnp.bfloat16)
    qv_wide = qvb.astype(jnp.float32)
    qkv_bias = jnp.concatenate([qv_wide[:width], jnp.zeros((width,), jnp.float32), qv_wide[width:]])
    qkv = jnp.dot(act1, qkv_full, preferred_element_type=jnp.float32) + qkv_bias
    queries = qkv[:, :width].astype(jnp.bfloat16).reshape(seqs_loc, rows_q, width)
    keys_loc = qkv[:, width : 2 * width].astype(jnp.bfloat16).reshape(seqs_loc, rows_q, width)
    values_loc = qkv[:, 2 * width :].astype(jnp.bfloat16).reshape(seqs_loc, rows_q, width)
    keys_all, values_all = (
        lax.all_gather(keys_loc, "context", axis=1, tiled=True),
        lax.all_gather(values_loc, "context", axis=1, tiled=True),
    )
    keys_len = keys_all.shape[1]
    q_start = lax.axis_index("context") * rows_q
    scores = masked_scores(queries, keys_all, q_start)
    top = jnp.max(scores, -1, keepdims=True)
    lse = top + jnp.log(jnp.sum(jnp.exp(scores - top), -1, keepdims=True))
    probs = jnp.exp(scores - lse).astype(jnp.bfloat16)
    attended = jnp.einsum(
        "shqk,skhd->sqhd", probs, split_heads(values_all), preferred_element_type=jnp.float32
    )
    attended = attended.reshape(-1, width).astype(jnp.bfloat16)
    resid = (
        rows
        + jnp.dot(attended, out_full, preferred_element_type=jnp.float32)
        + outb.astype(jnp.float32)
    )
    normed2, rstd2, pre2 = norm_fwd(resid, gain2, shift2)
    act2 = pre2.astype(jnp.bfloat16).reshape(seqs_loc, rows_q, width)
    act2_all = lax.all_gather(act2, "tensor", axis=0, tiled=True).reshape(-1, width)
    pre = jnp.dot(act2_all, up_full, preferred_element_type=jnp.float32) + upb
    hval, slope = gelu_pair(pre)
    hidden = hval.astype(jnp.bfloat16)
    partial_out = jnp.dot(hidden, down_full, preferred_element_type=jnp.float32).reshape(
        -1, rows_q, width
    )
    mlp_out = (
        lax.psum_scatter(
            partial_out.astype(jnp.bfloat16), "tensor", scatter_dimension=0, tiled=True
        )
        .astype(jnp.float32)
        .reshape(-1, width)
    )
    block_out = resid + mlp_out + downb.astype(jnp.float32)
    cot = cotangent.reshape(-1, width)
    g_down_bias = jnp.sum(cot, 0)
    cot_all = lax.all_gather(cotangent.astype(jnp.bfloat16), "tensor", axis=0, tiled=True).reshape(
        -1, width
    )
    up_back, down_back = (up_full, down_full)
    qkv_back, out_back = (qkv_full, out_full)
    g_down_t = jnp.dot(cot_all.T, hidden, preferred_element_type=jnp.float32)
    pre_grad = jnp.dot(cot_all, down_back.T, preferred_element_type=jnp.float32) * slope
    g_up_loc = jnp.sum(pre_grad, 0)
    pre_low = pre_grad.astype(jnp.bfloat16)
    g_up = jnp.dot(act2_all.T, pre_low, preferred_element_type=jnp.float32)
    act2_part = jnp.dot(pre_low, up_back.T, preferred_element_type=jnp.float32).reshape(
        -1, rows_q, width
    )
    act2_grad = (
        lax.psum_scatter(act2_part.astype(jnp.bfloat16), "tensor", scatter_dimension=0, tiled=True)
        .astype(jnp.float32)
        .reshape(-1, width)
    )
    g_gain2 = jnp.sum(act2_grad * normed2, 0)
    g_shift2 = jnp.sum(act2_grad, 0)
    resid_grad = cot + norm_back(act2_grad * gain2.astype(jnp.float32), normed2, rstd2)
    g_out_bias = jnp.sum(resid_grad, 0)
    resid_low = resid_grad.astype(jnp.bfloat16)
    g_out = jnp.dot(attended.T, resid_low, preferred_element_type=jnp.float32)
    attended_grad = jnp.dot(resid_low, out_back.T, preferred_element_type=jnp.float32).astype(
        jnp.bfloat16
    )
    attended_grad = attended_grad.reshape(seqs_loc, rows_q, width)
    pf = jnp.exp(masked_scores(queries, keys_all, q_start) - lse)
    probs_low = pf.astype(jnp.bfloat16)
    dprobs = jnp.einsum(
        "sqhd,skhd->shqk",
        split_heads(attended_grad),
        split_heads(values_all),
        preferred_element_type=jnp.float32,
    )
    delta = jnp.sum(pf * dprobs, -1, keepdims=True)
    dscore = (pf * (dprobs - delta)).astype(jnp.bfloat16)
    scale = HEAD_DIM ** (-0.5)
    query_grad = (
        jnp.einsum(
            "shqk,skhd->sqhd", dscore, split_heads(keys_all), preferred_element_type=jnp.float32
        )
        * scale
    )
    key_full = (
        jnp.einsum(
            "shqk,sqhd->skhd", dscore, split_heads(queries), preferred_element_type=jnp.float32
        )
        * scale
    )
    value_full = jnp.einsum(
        "shqk,sqhd->skhd", probs_low, split_heads(attended_grad), preferred_element_type=jnp.float32
    )
    kv_full = jnp.concatenate(
        [
            key_full.reshape(seqs_loc, keys_len, width),
            value_full.reshape(seqs_loc, keys_len, width),
        ],
        2,
    )
    kv_grad = lax.psum_scatter(
        kv_full.astype(jnp.bfloat16), "context", scatter_dimension=1, tiled=True
    ).astype(jnp.float32)
    query_grad = query_grad.reshape(-1, width)
    key_grad = kv_grad[:, :, :width].reshape(-1, width)
    value_grad = kv_grad[:, :, width:].reshape(-1, width)
    g_qv_bias = jnp.concatenate([jnp.sum(query_grad, 0), jnp.sum(value_grad, 0)])
    qkv_low = jnp.concatenate([query_grad, key_grad, value_grad], 1).astype(jnp.bfloat16)
    g_qkv = jnp.dot(act1.T, qkv_low, preferred_element_type=jnp.float32)
    act1_grad = jnp.dot(qkv_low, qkv_back.T, preferred_element_type=jnp.float32)
    g_gain1 = jnp.sum(act1_grad * normed1, 0)
    g_shift1 = jnp.sum(act1_grad, 0)
    input_grad = resid_grad + norm_back(act1_grad * gain1.astype(jnp.float32), normed1, rstd1)
    g_up_bias = lax.dynamic_update_slice_in_dim(
        jnp.zeros((upb_all.shape[0],), jnp.float32), g_up_loc, tensor_pos * hidden_loc, 0
    )
    small_cols = jnp.stack([g_gain1, g_shift1, g_out_bias, g_gain2, g_shift2, g_down_bias], 1)
    attn_stack = jnp.concatenate(
        [g_qkv, g_out, small_cols, g_qv_bias.reshape(width, 2), g_up_bias.reshape(width, -1)], 1
    )
    mlp_stack = jnp.concatenate([g_up, g_down_t], 1)
    s_attn = lax.psum_scatter(
        attn_stack.astype(jnp.bfloat16), ("shard", "tensor"), scatter_dimension=0, tiled=True
    )
    s_mlp = lax.psum_scatter(
        mlp_stack.astype(jnp.bfloat16), "shard", scatter_dimension=0, tiled=True
    )
    t_attn, t_mlp = (
        lax.psum(s_attn, "context").astype(jnp.float32),
        lax.psum(s_mlp, "context").astype(jnp.float32),
    )
    base = 4 * width
    t_qkv = t_attn[:, : 3 * width]
    t_out = t_attn[:, 3 * width : base]
    t_gain1 = t_attn[:, base]
    t_shift1 = t_attn[:, base + 1]
    t_outb = t_attn[:, base + 2]
    t_gain2 = t_attn[:, base + 3]
    t_shift2 = t_attn[:, base + 4]
    t_downb = t_attn[:, base + 5]
    t_qvb = t_attn[:, base + 6 : base + 8].reshape(-1)
    t_upb = t_attn[:, base + 8 :].reshape(-1)
    t_up = t_mlp[:, :hidden_loc]
    t_down = t_mlp[:, hidden_loc:].T
    return (
        block_out.reshape(seqs_loc, rows_q, width),
        input_grad.reshape(seqs_loc, rows_q, width),
        t_qkv,
        t_out,
        t_up,
        t_down,
        t_gain1,
        t_shift1,
        t_qvb,
        t_outb,
        t_gain2,
        t_shift2,
        t_upb,
        t_downb,
    )


def swap(value, axis, size, bit=1):
    return lax.ppermute(value, axis, [(i, i ^ bit) for i in range(size)])


def pick(value, index, dim):
    return lax.dynamic_index_in_dim(value, index, dim, keepdims=False)


def wide(value):
    return value.astype(jnp.float32)


def halve(value, dim, axis, size, bit=1):
    mine = (lax.axis_index(axis) // bit) % 2
    got = swap(pick(value, 1 - mine, dim), axis, size, bit)
    return (wide(pick(value, mine, dim)) + wide(got)).astype(value.dtype)


def pair(first, second, flag, dim):
    return jnp.where(
        flag == 0, jnp.concatenate([first, second], dim), jnp.concatenate([second, first], dim)
    )


def reduce_owned(grad, shards, context_first):
    blocks, keep_rows, cols = grad.shape
    stages = shards.bit_length() - 1
    grad = grad.reshape(*([2] * stages), 2, 2, keep_rows, cols)
    grad = halve(grad, stages, "tensor", 2)
    if context_first:
        grad = halve(grad, stages, "context", 2)
        grad = halve(grad, stages - 1, "shard", shards)
    else:
        grad = halve(grad, stages - 1, "shard", shards)
        grad = halve(grad, stages - 1, "context", 2)
    for left in range(stages - 1, 0, -1):
        grad = halve(grad, 0, "shard", shards, 2**left)
    return grad


def whole_rows(part, rows, flag):
    part = part[:rows]
    return wide(pair(part, swap(part, "context", 2), flag, 0))


def on_device_pairs(
    shards,
    block_in,
    cotangent,
    qkv_weight,
    out_weight,
    up_weight,
    down_weight,
    ln1_gain,
    ln1_bias,
    qv_bias,
    out_bias,
    ln2_gain,
    ln2_bias,
    up_bias,
    down_bias,
):
    f32, bf16 = jnp.float32, jnp.bfloat16
    _, rows_half, width = block_in.shape
    length = 2 * rows_half
    owners = 2 * shards
    own = width // owners
    ctx, tpos, spos = (lax.axis_index(a) for a in ("context", "tensor", "shard"))
    dot = functools.partial(jnp.dot, preferred_element_type=f32)

    def to_sequence(value):
        return pair(pick(value, ctx, 0), swap(pick(value, 1 - ctx, 0), "context", 2), ctx, 0)

    def from_sequence(value):
        value = value.reshape(2, rows_half, width)
        mine, got = pick(value, ctx, 0), swap(pick(value, 1 - ctx, 0).astype(bf16), "context", 2)
        return pair(mine[None], got[None].astype(f32), ctx, 0)

    smalls = [ln1_gain, ln1_bias, out_bias, ln2_gain, ln2_bias, down_bias, qv_bias, up_bias]
    small = jnp.concatenate(smalls)
    small = jnp.pad(small, (0, qkv_weight.shape[1] - small.shape[0]))[None]
    packed = jnp.concatenate([qkv_weight, small], 0)[None]
    packed_all = lax.all_gather(packed, ("shard", "tensor"), axis=0, tiled=True)
    rows = to_sequence(block_in)
    hid = up_weight.shape[1] // 2
    up_part = lax.dynamic_slice_in_dim(up_weight, ctx * hid, hid, 1)
    down_part = lax.dynamic_slice_in_dim(down_weight, ctx * hid, hid, 0).T
    down_t = down_part
    bits = [shards >> k for k in range(1, shards.bit_length())]
    for bit in bits:
        if bit == 1:
            packed_all, down_t = lax.optimization_barrier((packed_all, down_t))
        got = swap(down_t, "shard", shards, bit)
        down_t = pair(down_t[None], got[None], (spos // bit) % 2, 0)
    order = list(range(len(bits)))[::-1] + [len(bits), len(bits) + 1]
    out_weight, packed_all = lax.optimization_barrier((out_weight, packed_all))
    out_mine = lax.all_gather(out_weight[None], "shard", axis=0, tiled=True)
    out_full = pair(out_mine[:, None], swap(out_mine, "tensor", 2)[:, None], tpos, 1)
    out_full = out_full.reshape(width, width)
    up_part, out_mine = lax.optimization_barrier((up_part, out_mine))
    up_full = lax.all_gather(up_part, "shard", axis=0, tiled=True)
    qkv_full = packed_all[:, :own].reshape(width, -1)
    small_all = packed_all[:, own]
    gathered, at = [], 0
    for s in smalls:
        gathered.append(small_all[:, at : at + s.shape[0]].reshape(-1))
        at += s.shape[0]
    gain1, shift1, outb, gain2, shift2, downb, qvb, upb_all = gathered
    upb = wide(lax.dynamic_slice_in_dim(upb_all, (tpos * 2 + ctx) * hid, hid))

    normed1, rstd1, pre1 = norm_fwd(rows, gain1, shift1)
    act1 = pre1.astype(bf16)
    qv_wide = wide(qvb)
    qkv_bias = jnp.concatenate([qv_wide[:width], jnp.zeros((width,), f32), qv_wide[width:]])
    qkv = (dot(act1, qkv_full) + qkv_bias).astype(bf16)
    queries = qkv[None, :, :width]
    keys = qkv[None, :, width : 2 * width]
    values = qkv[None, :, 2 * width :]
    scores = masked_scores(queries, keys, 0)
    top = jnp.max(scores, -1, keepdims=True)
    lse = top + jnp.log(jnp.sum(jnp.exp(scores - top), -1, keepdims=True))
    probs = jnp.exp(scores - lse).astype(bf16)
    attended = jnp.einsum("shqk,skhd->sqhd", probs, split_heads(values), preferred_element_type=f32)
    attended = attended.reshape(-1, width).astype(bf16)
    attended, down_t = lax.optimization_barrier((attended, down_t))
    down_t = down_t.transpose(order).reshape(width, hid)
    resid = rows + dot(attended, out_full) + wide(outb)
    normed2, rstd2, pre2 = norm_fwd(resid, gain2, shift2)

    def spread(value):
        near = jnp.concatenate([value, swap(value, "tensor", 2)], 0)
        far = swap(value, "context", 2)
        return near, jnp.concatenate([far, swap(far, "tensor", 2)], 0)

    def collect(near, far):
        near, far = near.reshape(2, length, width), far.reshape(2, length, width)
        far = far[0] + wide(swap(far[1].astype(bf16), "tensor", 2))
        far = wide(swap(far.astype(bf16), "context", 2))
        return near[0] + wide(swap(near[1].astype(bf16), "tensor", 2)) + far

    def against(left, right):
        return lax.dot_general(left, right, (((1,), (1,)), ((), ())), preferred_element_type=f32)

    def over_tokens(left, right):
        return lax.dot_general(left, right, (((0,), (0,)), ((), ())), preferred_element_type=f32)

    cot = to_sequence(cotangent)
    cot_sets = spread(cot.astype(bf16))
    act2_sets = spread(pre2.astype(bf16))
    hiddens, slopes = [], []
    for act in act2_sets:
        hval, slope = gelu_pair(dot(act, up_full) + upb)
        hiddens.append(hval.astype(bf16))
        slopes.append(slope)
    pre_grads = [dot(c, down_t) * s for c, s in zip(cot_sets, slopes)]
    g_up_loc = sum(jnp.sum(p, 0) for p in pre_grads)
    pre_lows = [p.astype(bf16) for p in pre_grads]
    act2_grad = collect(*[against(p, up_full) for p in pre_lows])
    cot_cat = jnp.concatenate(cot_sets, 0)
    act2_cat = jnp.concatenate(act2_sets, 0)
    g_down_t = over_tokens(cot_cat, jnp.concatenate(hiddens, 0)).astype(bf16)
    g_up = over_tokens(act2_cat, jnp.concatenate(pre_lows, 0)).astype(bf16)
    s_down = lax.psum_scatter(g_down_t, "shard", scatter_dimension=0, tiled=True)
    s_up = lax.psum_scatter(g_up, "shard", scatter_dimension=0, tiled=True)
    mlp_out = collect(*[against(h, down_t) for h in hiddens])
    block_out = from_sequence(resid + mlp_out + wide(downb))

    g_down_bias = jnp.sum(cot, 0)
    g_gain2 = jnp.sum(act2_grad * normed2, 0)
    g_shift2 = jnp.sum(act2_grad, 0)
    resid_grad = cot + norm_back(act2_grad * wide(gain2), normed2, rstd2)
    g_out_bias = jnp.sum(resid_grad, 0)
    resid_low = resid_grad.astype(bf16)
    half = own // 2

    def in_blocks(value, count):
        value = value.reshape(length, -1, count)
        return jnp.pad(value, ((0, 0), (0, 0), (0, -count % 8))).reshape(length, -1)

    def owned(left, right, context_first):
        grad = over_tokens(in_blocks(left, half), right).astype(bf16)
        return reduce_owned(grad.reshape(2 * owners, -1, grad.shape[1]), shards, context_first)

    s_out = owned(attended, resid_low, True)
    attended_grad = against(resid_low, out_full).astype(bf16)[None]
    pf = jnp.exp(masked_scores(queries, keys, 0) - lse)
    probs_low = pf.astype(bf16)
    dprobs = jnp.einsum(
        "sqhd,skhd->shqk",
        split_heads(attended_grad),
        split_heads(values),
        preferred_element_type=f32,
    )
    delta = jnp.sum(pf * dprobs, -1, keepdims=True)
    dscore = (pf * (dprobs - delta)).astype(bf16)
    scale = HEAD_DIM ** (-0.5)
    query_grad = scale * jnp.einsum(
        "shqk,skhd->sqhd", dscore, split_heads(keys), preferred_element_type=f32
    )
    key_grad = scale * jnp.einsum(
        "shqk,sqhd->skhd", dscore, split_heads(queries), preferred_element_type=f32
    )
    value_grad = jnp.einsum(
        "shqk,sqhd->skhd", probs_low, split_heads(attended_grad), preferred_element_type=f32
    )
    query_grad, key_grad, value_grad = (
        g.reshape(-1, width) for g in (query_grad, key_grad, value_grad)
    )
    g_qv_bias = jnp.concatenate([jnp.sum(query_grad, 0), jnp.sum(value_grad, 0)])
    qkv_low = jnp.concatenate([query_grad, key_grad, value_grad], 1).astype(bf16)
    cut = -(-qkv_low.shape[1] // 256) * 128
    qkv_low, s_out = lax.optimization_barrier((qkv_low, s_out))
    s_qkv = [owned(act1, qkv_low[:, :cut], False), owned(act1, qkv_low[:, cut:], True)]
    act1_grad = against(qkv_low, qkv_full)
    g_gain1 = jnp.sum(act1_grad * normed1, 0)
    g_shift1 = jnp.sum(act1_grad, 0)
    input_grad = resid_grad + norm_back(act1_grad * wide(gain1), normed1, rstd1)
    input_grad = from_sequence(input_grad)
    g_up_bias = lax.dynamic_update_slice_in_dim(
        jnp.zeros((upb_all.shape[0],), f32), g_up_loc, (tpos * 2 + ctx) * hid, 0
    )
    g_smalls = [
        g_gain1, g_shift1, g_out_bias, g_gain2, g_shift2, g_down_bias, g_qv_bias, g_up_bias
    ]
    g_small = jnp.concatenate([g.reshape(owners, -1) for g in g_smalls], 1)
    g_small = reduce_owned(g_small.reshape(2 * owners, 1, -1), shards, True)
    g_small = whole_rows(g_small, 1, ctx).reshape(-1)
    t_small, at = [], 0
    for s in smalls:
        t_small.append(g_small[at : at + s.shape[0]])
        at += s.shape[0]
    t_gain1, t_shift1, t_outb, t_gain2, t_shift2, t_downb, t_qvb, t_upb = t_small
    t_qkv = jnp.concatenate([whole_rows(s, half, ctx) for s in s_qkv], 1)
    t_out = whole_rows(s_out, half, ctx)
    t_up = wide(pair(s_up, swap(s_up, "context", 2), ctx, 1))
    t_down = wide(pair(s_down, swap(s_down, "context", 2), ctx, 1)).T
    return (
        block_out,
        input_grad,
        t_qkv,
        t_out,
        t_up,
        t_down,
        t_gain1,
        t_shift1,
        t_qvb,
        t_outb,
        t_gain2,
        t_shift2,
        t_upb,
        t_downb,
    )


def device_step(mesh):
    shards = mesh.shape["shard"]
    paired = mesh.shape["context"] == 2 and mesh.shape["tensor"] == 2
    paired = paired and shards > 1 and shards & (shards - 1) == 0

    def step(block_in, *rest):
        width = block_in.shape[2]
        if paired and block_in.shape[0] == 2 and width % (4 * shards) == 0:
            return on_device_pairs(shards, block_in, *rest)
        return on_device(block_in, *rest)

    return step


def solution(mesh):
    return jax.shard_map(
        device_step(mesh),
        mesh=mesh,
        in_specs=(
            P(("shard", "tensor"), "context", None),
            P(("shard", "tensor"), "context", None),
            P(("shard", "tensor"), None),
            P(("shard", "tensor"), None),
            P("shard", "tensor"),
            P("tensor", "shard"),
            P(("shard", "tensor")),
            P(("shard", "tensor")),
            P(("shard", "tensor")),
            P(("shard", "tensor")),
            P(("shard", "tensor")),
            P(("shard", "tensor")),
            P(("shard", "tensor")),
            P(("shard", "tensor")),
        ),
        out_specs=(
            P(("shard", "tensor"), "context", None),
            P(("shard", "tensor"), "context", None),
            P(("shard", "tensor"), None),
            P(("shard", "tensor"), None),
            P("shard", "tensor"),
            P("tensor", "shard"),
            P(("shard", "tensor")),
            P(("shard", "tensor")),
            P(("shard", "tensor")),
            P(("shard", "tensor")),
            P(("shard", "tensor")),
            P(("shard", "tensor")),
            P(("shard", "tensor")),
            P(("shard", "tensor")),
        ),
        check_vma=False,
    )
```
